32 devices in a mesh: order: 4 (over z), band: 4 (over x, core), chan: 2 (over y).
Axes of the slice: x: 2, y: 2, z: 4, core: 2. Of those that a mesh axis runs over, the one named last changes fastest.
Arguments:
- coef_grad: bfloat16 [2, 368, 2, 384, 361], P('chan', ('order', 'band')), may hold values from -6 to 6
- coef_saved: bfloat16 [2, 368, 2, 73, 361], P('chan', ('order', 'band')), may hold values from -0.016601562 to 0.016601562
- lift_weight: bfloat16 [384, 73], replicated, may hold values from -0.3125 to 0.3125
- legendre: bfloat16 [368, 361, 16], P(('order', 'band')), may hold values from -0.3125 to 0.3125
- order_of_slot: int32 [368], replicated, may hold values from 0 to 367, as said below
- trunc_degree: int32 [2], P('chan'), may hold values from 271 to 360
Outputs:
- grid_grad: bfloat16 [2, 73, 16, 1440], P('chan', None, ('order', 'band'))
- weight_grad: float32 [384, 73], P(('order', 'band'))
The draws below stay inside these ranges and needn't reach their ends.
Inputs may be any that keep to these rules, and one draw needn't show every extreme that they name: order_of_slot holds each of 0 to 367 once; in the g-th block of 23 slots, slot s holds s * 16 + k_g for even s and s * 16 + 15 - k_g for odd s, where k is a permutation of 0 to 15.
All inputs are finite; a program needn't handle non-finite values.
Results may differ from the reference program's by a relative error of at most 0.0062.
Values may be sent and summed in bfloat16 or wider, within the bound.
No kernel may reach another device: no remote copies, remote signals or barrier semaphores. Data moves between devices by JAX's collectives and lax.ppermute only.
A program may use at most 64 MiB of HBM per device.

```python
import math
import jax
import jax.numpy as jnp
from jax import lax

C_IN = 73
EMBED = 384
L = 361
LON = 1440
GROUPS = 16
SLOTS_DEV = 23
SLOTS = 368
SAMP = 2
LAT = 16


def draw_order_of_slot(key, part):
    shuffled = jax.random.permutation(key, GROUPS).astype(jnp.int32)
    slot_ids = jnp.arange(SLOTS_DEV, dtype=jnp.int32)
    rising = slot_ids[None, :] * GROUPS + shuffled[:, None]
    falling = slot_ids[None, :] * GROUPS + (GROUPS - 1 - shuffled[:, None])
    orders = jnp.where(slot_ids[None, :] % 2 == 0, rising, falling)
    return orders.reshape(GROUPS * SLOTS_DEV).astype(jnp.int32)


def steps_of(key, extent, pieces, low, high):
    level, own = 1.0, jax.random.fold_in(key, 6)
    for position, parts in pieces:
        draws = jnp.exp(jax.random.uniform(jax.random.fold_in(own, position), (parts,), jnp.float32, low / len(pieces), high / len(pieces)))
        level = level * jnp.repeat(draws, extent[position] // parts).reshape([-1 if axis == position else 1 for axis in range(len(extent))])
    return level


def centred(own_key, extent, spread, limit, shards=(), kind=jnp.bfloat16):
    array = jax.random.normal(own_key, extent, jnp.float32) * spread
    if len(shards) > 0:
        array = steps_of(own_key, extent, shards, -0.22, 0.18) * array
    return jnp.clip(array, min=-limit, max=limit).astype(kind)


def setup_inputs(seed: int = 0) -> dict:
    streams_of = jax.random.split(jax.random.key(seed), 7)
    coef_grad = centred(streams_of[0], (SAMP, SLOTS, 2, EMBED, L), 1.0, 6.0, ((0, 2), (1, 16)))
    coef_saved = centred(streams_of[1], (SAMP, SLOTS, 2, C_IN, L), (1.0 / L), 0.016601562, ((0, 2), (1, 16)))
    lift_weight = centred(streams_of[2], (EMBED, C_IN), EMBED ** -0.5, 0.3125)
    legendre = centred(streams_of[3], (SLOTS, L, LAT), L ** -0.5, 0.3125, ((0, 16),))
    order_of_slot = draw_order_of_slot(jax.random.fold_in(streams_of[6], 71), 0)
    trunc_degree = jax.random.randint(streams_of[5], (SAMP,), L - L // 4, L).astype(jnp.int32)
    return dict(coef_grad=coef_grad, coef_saved=coef_saved, lift_weight=lift_weight, legendre=legendre, order_of_slot=order_of_slot, trunc_degree=trunc_degree)


def reference(coef_grad, coef_saved, lift_weight, legendre, order_of_slot, trunc_degree):
    degree_ids = jnp.arange(L, dtype=jnp.int32)
    weight_wide = lift_weight.astype(jnp.float32)
    lon_ids = jnp.arange(LON, dtype=jnp.int32)
    angles = (order_of_slot[:, None] * lon_ids[None, :] % LON).astype(jnp.float32) * (2.0 * math.pi / LON)
    angle_table = jnp.stack([jnp.cos(angles), -jnp.sin(angles)], axis=1).astype(jnp.bfloat16)
    angle_table = lax.optimization_barrier(angle_table).astype(jnp.float32)
    legendre_wide = legendre.astype(jnp.float32)
    synth_scale = 1.0 / math.sqrt(LON)

    def one_sample(inputs):
        grad_one, saved_one, top_degree = inputs
        live_mask = (degree_ids[None, :] >= order_of_slot[:, None]) & (degree_ids[None, :] <= top_degree)
        kept_grad = jnp.where(live_mask[:, None, None, :], grad_one, jnp.zeros((), grad_one.dtype))
        kept_wide = kept_grad.astype(jnp.float32)
        saved_wide = saved_one.astype(jnp.float32)
        grad_terms = jnp.einsum('qrel,qrcl->ec', kept_wide, saved_wide)
        lifted = jnp.einsum('qrel,ec->qrcl', kept_wide, weight_wide)
        lifted = lax.optimization_barrier(lifted.astype(jnp.bfloat16)).astype(jnp.float32)
        lifted = lifted.reshape(SLOTS, 2 * C_IN, L)
        spectral = jnp.einsum('qlt,qjl->qtj', legendre_wide, lifted).astype(jnp.bfloat16)
        spectral = lax.optimization_barrier(spectral).astype(jnp.float32)
        split_parts = spectral.reshape(SLOTS, LAT, 2, C_IN)
        synth_field = jnp.einsum('qtrc,qrn->ctn', split_parts, angle_table) * synth_scale
        return (synth_field.astype(jnp.bfloat16), grad_terms)
    grid_grad, weight_terms = lax.map(one_sample, (coef_grad, coef_saved, trunc_degree))
    return (grid_grad, lax.optimization_barrier(jnp.sum(weight_terms, axis=0)))
```

```python
import math

import jax
import jax.numpy as jnp
from jax import lax
from jax.experimental import pallas as pl
from jax.experimental.pallas import tpu as pltpu
from jax.sharding import PartitionSpec as P

LON = 1440
LANES = 128
GROUP_AXES = ("order", "band")


def round_up(value, step):
    return -(-value // step) * step


def slot_classes(slots, groups, degrees):
    classes = {}
    for slot in range(slots):
        low = groups * slot
        if low < degrees:
            classes.setdefault(low // LANES, []).append(slot)
    return [(tile, found[0], found[-1] + 1) for tile, found in sorted(classes.items())]


def lane_tiles(degrees):
    return [(at, min(LANES, degrees - at)) for at in range(0, degrees, LANES)]


def spectral_kernel(groups, pad_slots, order_hbm, trunc_hbm, grad_hbm, saved_hbm, legendre_hbm, weight_hbm,
                    out_ref, order_ref, trunc_ref, legendre_buf, weight_buf, grad_buf, *rest):
    slots, degrees, _, embed = grad_hbm.shape
    chan_in = weight_hbm.shape[0]
    chan_pad = round_up(chan_in, 8)
    lats = legendre_hbm.shape[1]
    tiles = lane_tiles(degrees)
    saved_bufs = rest[: len(tiles)]
    grad_wide, saved_wide, spec_wide, weight_acc, weight_turned, small_sem, grad_sem, saved_sem = rest[len(tiles):]
    small_copies = [
        pltpu.make_async_copy(source, target, small_sem.at[at])
        for at, (source, target) in enumerate([
            (order_hbm, order_ref), (trunc_hbm, trunc_ref), (legendre_hbm, legendre_buf), (weight_hbm, weight_buf)
        ])
    ]
    for copy in small_copies:
        copy.start()
    embed_tiles = embed // LANES
    classes = slot_classes(slots, groups, degrees)

    def grad_copies(slot, tile):
        rows = pl.ds(tile * LANES, degrees - tile * LANES)
        return [
            pltpu.make_async_copy(
                grad_hbm.at[slot, rows, :, pl.ds(at * LANES, LANES)],
                grad_buf.at[slot, at, rows],
                grad_sem.at[slot, at],
            )
            for at in range(embed_tiles)
        ]

    def saved_copies(slot, tile):
        return [
            pltpu.make_async_copy(
                saved_hbm.at[slot, :, :, pl.ds(*tiles[at])],
                saved_bufs[at].at[slot, pl.ds(0, chan_in)],
                saved_sem.at[slot, at],
            )
            for at in range(tile, len(tiles))
        ]

    for tile, first, last in classes:
        @pl.loop(first, last)
        def _(slot):
            for copy in grad_copies(slot, tile) + saved_copies(slot, tile):
                copy.start()

    spec_wide[...] = jnp.zeros_like(spec_wide)
    weight_acc[...] = jnp.zeros_like(weight_acc)
    for at in range(embed_tiles):
        grad_wide[at, 2 * degrees // 8 * 8 :] = jnp.zeros((grad_wide.shape[1] - 2 * degrees // 8 * 8, LANES), jnp.float32)
    for copy in small_copies:
        copy.wait()
    first_slot = (lax.axis_index("order") * lax.axis_size("band") + lax.axis_index("band")) * slots
    top = trunc_ref[0]
    for tile, first, last in classes:
        low = tile * LANES
        live = degrees - low
        live_pad = round_up(live, LANES)

        @pl.loop(first, last)
        def _(slot):
            for copy in grad_copies(slot, tile) + saved_copies(slot, tile):
                copy.wait()
            order = order_ref[first_slot + slot]
            degree = lax.broadcasted_iota(jnp.int32, (1, live_pad), 1) + low
            mask = (degree >= order) & (degree <= top)
            for at in range(embed_tiles):
                pairs = grad_buf[slot, at, low:degrees].reshape(2 * live, LANES)
                grad_wide[at, : 2 * live] = pairs.astype(jnp.float32)
            for at in range(tile, len(tiles)):
                start, width = tiles[at]
                pairs = saved_bufs[at][slot, :chan_in].reshape(2 * chan_in, width)
                saved_wide[at, : 2 * chan_in, :width] = pairs.astype(jnp.float32)
            lat_rows = legendre_buf[slot, :, low:degrees]
            lat_rows = jnp.where(mask[:, :live], lat_rows.astype(jnp.float32), 0.0).astype(jnp.bfloat16)
            for part in range(2):
                grads = jnp.concatenate(
                    [grad_wide[at, pl.ds(part, live_pad, stride=2)].astype(jnp.bfloat16) for at in range(embed_tiles)],
                    axis=1,
                )
                saved = jnp.concatenate(
                    [saved_wide[at, pl.ds(part, chan_pad, stride=2)] for at in range(tile, len(tiles))], axis=1
                )
                saved = jnp.where(mask, saved, 0.0).astype(jnp.bfloat16)
                lifted = lax.dot_general(
                    grads, weight_buf[...], (((1,), (1,)), ((), ())), preferred_element_type=jnp.float32
                ).astype(jnp.bfloat16)
                spec = jnp.dot(lat_rows, lifted[:live], preferred_element_type=jnp.float32)
                row = pl.multiple_of((part * pad_slots + slot) * lats, lats)
                spec_wide[pl.ds(row, lats), :chan_in] = spec
                weight_acc[:chan_pad] += jnp.dot(saved, grads, preferred_element_type=jnp.float32)

    for at in range(embed_tiles):
        weight_turned[at * LANES : (at + 1) * LANES] = weight_acc[:, at * LANES : (at + 1) * LANES].T
    rows_dev = embed // groups
    head = LANES - chan_in
    lane = lax.broadcasted_iota(jnp.int32, (2 * pad_slots, LANES), 1)
    for group in range(groups):
        block = weight_turned[group * rows_dev : (group + 1) * rows_dev]
        shifted = [pltpu.roll(block, chan_in, 1), pltpu.roll(block, chan_in - head, 1)]
        if rows_dev < pad_slots:
            fill = jnp.zeros((pad_slots - rows_dev, LANES), jnp.float32)
            shifted = [shifted[0], fill, shifted[1], fill]
        spec = spec_wide[pl.ds(group, 2 * pad_slots, stride=lats)]
        both = jnp.where(lane < chan_in, spec, jnp.concatenate(shifted, axis=0))
        out_ref[group] = both.astype(jnp.bfloat16)


def table_kernel(groups, slots, order_ref, table_ref):
    pad_slots = table_ref.shape[0] // (2 * groups)
    shape = (pad_slots, LANES)
    slot = lax.broadcasted_iota(jnp.int32, shape, 0)
    lane = lax.broadcasted_iota(jnp.int32, shape, 1)

    def circle(steps):
        steps = steps.astype(jnp.float32)
        turns = jnp.floor(steps * (1.0 / LON) + 0.5)
        half = (steps - turns * LON) * (math.pi / LON)
        square = half * half
        sine = 1.0
        for power in (11, 9, 7, 5, 3):
            sine = 1.0 - square * sine * (1.0 / (power * (power - 1)))
        sine = sine * half
        cosine = 1.0
        for power in (12, 10, 8, 6, 4, 2):
            cosine = 1.0 - square * cosine * (1.0 / (power * (power - 1)))
        return 1.0 - 2.0 * sine * sine, 2.0 * sine * cosine

    @pl.loop(0, groups)
    def _(group):
        key = order_ref[group * slots]
        order = slot * groups + jnp.where(slot % 2 == 0, key, groups - 1 - key)
        cosine, sine = circle(order * lane)
        turn_cosine, turn_sine = circle(order * LANES)
        row = pl.multiple_of(group * 2 * pad_slots, 2 * pad_slots)
        for at in range(0, LON, LANES):
            width = min(LANES, LON - at)
            both = jnp.concatenate([cosine, -sine], axis=0).astype(jnp.bfloat16)
            table_ref[pl.ds(row, 2 * pad_slots), at : at + width] = both[:, :width]
            cosine, sine = (
                cosine * turn_cosine - sine * turn_sine,
                sine * turn_cosine + cosine * turn_sine,
            )


def weight_kernel(chan_in, rows_dev, items_ref, sum_ref):
    groups, rows, _ = items_ref.shape
    pad_slots = rows // 2
    total = items_ref[0].astype(jnp.float32)
    for group in range(1, groups):
        total = total + items_ref[group].astype(jnp.float32)
    head = LANES - chan_in
    lane = lax.broadcasted_iota(jnp.int32, (pad_slots, LANES), 1)
    near = pltpu.roll(total[:pad_slots], LANES - chan_in, 1)
    far = pltpu.roll(total[pad_slots:], LANES - (chan_in - head), 1)
    sum_ref[...] = jnp.where(lane < head, near, far)[:rows_dev, :chan_in]


def synthesis_kernel(items_ref, table_ref, field_ref):
    chan_in = field_ref.shape[0]
    groups, rows, _ = items_ref.shape
    items = items_ref[...].reshape(groups * rows, LANES)
    field = lax.dot_general(
        items, table_ref[...], (((0,), (0,)), ((), ())), preferred_element_type=jnp.float32
    )
    field_ref[...] = (field[:chan_in] * (1.0 / math.sqrt(LON))).astype(jnp.bfloat16)


def local(coef_grad, coef_saved, lift_weight, legendre, order_of_slot, trunc_degree):
    _, slots, _, embed, degrees = coef_grad.shape
    chan_in = coef_saved.shape[3]
    lats = legendre.shape[2]
    groups = lax.axis_size(GROUP_AXES)
    samples = lax.axis_size("chan")
    rows_dev = embed // groups
    pad_slots = max(round_up(slots, 8), round_up(rows_dev, 8))
    rows = 2 * pad_slots
    embed_tiles = embed // LANES
    tiles = lane_tiles(degrees)
    assert coef_grad.shape[0] == 1 and lats == groups and 2 * (LANES - chan_in) >= chan_in

    smem = pl.BlockSpec(memory_space=pltpu.SMEM)
    vmem = pl.BlockSpec(memory_space=pltpu.VMEM)
    hbm = pl.BlockSpec(memory_space=pltpu.HBM)
    grad_view = jnp.transpose(coef_grad[0], (0, 3, 1, 2))
    saved_view = jnp.transpose(coef_saved[0], (0, 2, 1, 3))
    packed = pl.pallas_call(
        lambda *refs: spectral_kernel(groups, pad_slots, *refs),
        out_shape=jax.ShapeDtypeStruct((groups, rows, LANES), jnp.bfloat16),
        in_specs=[hbm] * 6,
        out_specs=vmem,
        scratch_shapes=[
            pltpu.SMEM(order_of_slot.shape, jnp.int32),
            pltpu.SMEM(trunc_degree.shape, jnp.int32),
            pltpu.VMEM((slots, lats, degrees), jnp.bfloat16),
            pltpu.VMEM((chan_in, embed), jnp.bfloat16),
            pltpu.VMEM((slots, embed_tiles, round_up(degrees, 8), 2, LANES), jnp.bfloat16),
            *[pltpu.VMEM((slots, round_up(chan_in, 8), 2, width), jnp.bfloat16) for _, width in tiles],
            pltpu.VMEM((embed_tiles, 2 * round_up(degrees, LANES) + 8, LANES), jnp.float32),
            pltpu.VMEM((len(tiles), 2 * round_up(chan_in, 8) + 8, LANES), jnp.float32),
            pltpu.VMEM(((rows + 1) * lats, LANES), jnp.float32),
            pltpu.VMEM((LANES, embed), jnp.float32),
            pltpu.VMEM((embed, LANES), jnp.float32),
            pltpu.SemaphoreType.DMA((4,)),
            pltpu.SemaphoreType.DMA((slots, embed_tiles)),
            pltpu.SemaphoreType.DMA((slots, len(tiles))),
        ],
        compiler_params=pltpu.CompilerParams(vmem_limit_bytes=60 << 20),
        name="spectral",
    )(order_of_slot, trunc_degree, grad_view, saved_view, jnp.transpose(legendre, (0, 2, 1)), lift_weight.T)

    received = lax.all_to_all(packed, GROUP_AXES, split_axis=0, concat_axis=0, tiled=True)

    table = pl.pallas_call(
        lambda *refs: table_kernel(groups, slots, *refs),
        out_shape=jax.ShapeDtypeStruct((groups * rows, LON), jnp.bfloat16),
        in_specs=[smem],
        out_specs=vmem,
        cost_estimate=pl.CostEstimate(flops=20_000_000, bytes_accessed=groups * rows * LON * 2, transcendentals=0),
        name="table",
    )(order_of_slot)

    own = pl.pallas_call(
        lambda *refs: weight_kernel(chan_in, rows_dev, *refs),
        out_shape=jax.ShapeDtypeStruct((rows_dev, chan_in), jnp.float32),
        in_specs=[vmem],
        out_specs=vmem,
        name="weight_rows",
    )(received)
    if samples == 2:
        weight_grad = own + lax.ppermute(own, "chan", [(0, 1), (1, 0)])
    else:
        weight_grad = lax.psum(own, "chan")

    field = pl.pallas_call(
        synthesis_kernel,
        out_shape=jax.ShapeDtypeStruct((chan_in, LON), jnp.bfloat16),
        in_specs=[vmem, vmem],
        out_specs=vmem,
        cost_estimate=pl.CostEstimate(flops=2 * groups * rows * LANES * LON, bytes_accessed=groups * rows * LON * 2, transcendentals=0),
        name="synthesis",
    )(received, table)
    return (field[None, :, None, :], weight_grad)


def solution(mesh):
    return jax.shard_map(
        local,
        mesh=mesh,
        in_specs=(
            P("chan", GROUP_AXES, None, None, None),
            P("chan", GROUP_AXES, None, None, None),
            P(),
            P(GROUP_AXES, None, None),
            P(),
            P("chan"),
        ),
        out_specs=(P("chan", None, GROUP_AXES, None), P(GROUP_AXES, None)),
        check_vma=False,
    )
```

```python
import math

import jax
import jax.numpy as jnp
from jax import lax
from jax.experimental import pallas as pl
from jax.experimental.pallas import tpu as pltpu
from jax.sharding import PartitionSpec as P

LON = 1440
LANES = 128
UNROLL = 4
GROUP_AXES = ("order", "band")


def round_up(value, step):
    return -(-value // step) * step


def slot_classes(slots, groups, degrees):
    classes = {}
    for slot in range(slots):
        low = groups * slot
        if low < degrees:
            classes.setdefault(low // LANES, []).append(slot)
    return [(tile, found[0], found[-1] + 1) for tile, found in sorted(classes.items())]


def lane_tiles(degrees):
    return [(at, min(LANES, degrees - at)) for at in range(0, degrees, LANES)]


def spectral_kernel(groups, pad_slots, order_hbm, trunc_hbm, grad_hbm, saved_hbm, legendre_hbm, weight_hbm,
                    out_ref, order_ref, trunc_ref, legendre_buf, weight_buf, grad_buf, *rest):
    slots, degrees, _, embed = grad_hbm.shape
    chan_in = weight_hbm.shape[0]
    chan_pad = round_up(chan_in, 8)
    lats = legendre_hbm.shape[1]
    tiles = lane_tiles(degrees)
    saved_bufs = rest[: len(tiles)]
    grad_wides = rest[len(tiles) : len(tiles) + UNROLL]
    saved_wides = rest[len(tiles) + UNROLL : len(tiles) + 2 * UNROLL]
    legendre_wide, tilted, spec_wide, weight_acc, weight_turned, small_sem, grad_sem, saved_sem = rest[len(tiles) + 2 * UNROLL :]
    grad_pairs = grad_hbm.reshape(slots, 2 * degrees, embed)
    saved_pairs = saved_hbm.reshape(slots, 2 * chan_in, degrees)
    small_copies = [
        pltpu.make_async_copy(source, target, small_sem.at[at])
        for at, (source, target) in enumerate([
            (order_hbm, order_ref), (trunc_hbm, trunc_ref), (legendre_hbm, legendre_buf), (weight_hbm, weight_buf)
        ])
    ]
    for copy in small_copies:
        copy.start()
    embed_tiles = embed // LANES
    classes = slot_classes(slots, groups, degrees)[::-1]

    def grad_copies(slot, tile):
        rows = pl.ds(2 * tile * LANES, 2 * (degrees - tile * LANES))
        return [
            pltpu.make_async_copy(
                grad_pairs.at[slot, rows, pl.ds(at * LANES, LANES)],
                grad_buf.at[slot, at, rows],
                grad_sem.at[slot, at],
            )
            for at in range(embed_tiles)
        ]

    def saved_copies(slot, tile):
        return [
            pltpu.make_async_copy(
                saved_pairs.at[slot, :, pl.ds(*tiles[at])],
                saved_bufs[at].at[slot, pl.ds(0, 2 * chan_in)],
                saved_sem.at[slot, at],
            )
            for at in range(tile, len(tiles))
        ]

    for tile, first, last in classes:
        @pl.loop(first, last)
        def _(slot):
            for copy in grad_copies(slot, tile) + saved_copies(slot, tile):
                copy.start()

    weight_acc[...] = jnp.zeros_like(weight_acc)
    tilted[...] = jnp.zeros_like(tilted)
    for wide in grad_wides:
        for at in range(embed_tiles):
            edge = 2 * degrees // 8 * 8
            wide[at, edge:] = jnp.zeros((wide.shape[1] - edge, LANES), jnp.float32)
    for copy in small_copies:
        copy.wait()
    first_slot = (lax.axis_index("order") * lax.axis_size("band") + lax.axis_index("band")) * slots
    top = trunc_ref[0]

    def run(slot_ids, tile):
        low = tile * LANES
        live = degrees - low
        live_pad = round_up(live, LANES)
        for slot in slot_ids:
            for copy in grad_copies(slot, tile) + saved_copies(slot, tile):
                copy.wait()
        total = None
        for at_slot, slot in enumerate(slot_ids):
            grad_wide, saved_wide = grad_wides[at_slot], saved_wides[at_slot]
            order = order_ref[first_slot + slot]
            degree = lax.broadcasted_iota(jnp.int32, (1, live_pad), 1) + low
            mask = (degree >= order) & (degree <= top)
            for at in range(embed_tiles):
                pairs = grad_buf[slot, at, 2 * low : 2 * degrees]
                grad_wide[at, : 2 * live] = pairs.astype(jnp.float32)
            for at in range(tile, len(tiles)):
                start, width = tiles[at]
                pairs = saved_bufs[at][slot, : 2 * chan_in]
                saved_wide[at, : 2 * chan_in, :width] = pairs.astype(jnp.float32)
                legendre_wide[at_slot, at, :, :width] = legendre_buf[slot, :, start : start + width].astype(jnp.float32)
            for part in range(2):
                grads = jnp.concatenate(
                    [grad_wide[at, pl.ds(part, live_pad, stride=2)].astype(jnp.bfloat16) for at in range(embed_tiles)],
                    axis=1,
                )
                left = jnp.concatenate(
                    [
                        jnp.concatenate(
                            [legendre_wide[at_slot, at], saved_wide[at, pl.ds(part, chan_pad, stride=2)]], axis=0
                        )
                        for at in range(tile, len(tiles))
                    ],
                    axis=1,
                )
                left = jnp.where(mask, left, 0.0).astype(jnp.bfloat16)
                both = jnp.dot(left, grads, preferred_element_type=jnp.float32)
                row = pl.multiple_of((part * pad_slots + slot) * lats, lats)
                tilted[pl.ds(row, lats)] = both[:lats].astype(jnp.bfloat16)
                total = both[lats:] if total is None else total + both[lats:]
        weight_acc[:chan_pad] += total

    for tile, first, last in classes:
        count = len(grad_wides)
        chunks = (last - first) // count

        @pl.loop(0, chunks)
        def _(chunk):
            run([first + chunk * count + at for at in range(count)], tile)

        if first + chunks * count < last:
            run(list(range(first + chunks * count, last)), tile)

    spec_wide[pl.ds(0, tilted.shape[0]), :chan_in] = lax.dot_general(
        tilted[...], weight_buf[...], (((1,), (1,)), ((), ())), preferred_element_type=jnp.float32
    )
    for at in range(embed_tiles):
        weight_turned[at * LANES : (at + 1) * LANES] = weight_acc[:, at * LANES : (at + 1) * LANES].T
    rows_dev = embed // groups
    head = LANES - chan_in
    lane = lax.broadcasted_iota(jnp.int32, (2 * pad_slots, LANES), 1)
    for group in range(groups):
        block = weight_turned[group * rows_dev : (group + 1) * rows_dev]
        shifted = [pltpu.roll(block, chan_in, 1), pltpu.roll(block, chan_in - head, 1)]
        if rows_dev < pad_slots:
            fill = jnp.zeros((pad_slots - rows_dev, LANES), jnp.float32)
            shifted = [shifted[0], fill, shifted[1], fill]
        spec = spec_wide[pl.ds(group, 2 * pad_slots, stride=lats)]
        both = jnp.where(lane < chan_in, spec, jnp.concatenate(shifted, axis=0))
        out_ref[group] = both.astype(jnp.bfloat16)


def table_kernel(groups, slots, order_ref, table_ref):
    pad_slots = table_ref.shape[0] // (2 * groups)
    shape = (pad_slots, LANES)
    slot = lax.broadcasted_iota(jnp.int32, shape, 0)
    lane = lax.broadcasted_iota(jnp.int32, shape, 1)

    def circle(steps):
        steps = steps.astype(jnp.float32)
        turns = jnp.floor(steps * (1.0 / LON) + 0.5)
        half = (steps - turns * LON) * (math.pi / LON)
        square = half * half
        sine = 1.0
        for power in (11, 9, 7, 5, 3):
            sine = 1.0 - square * sine * (1.0 / (power * (power - 1)))
        sine = sine * half
        cosine = 1.0
        for power in (12, 10, 8, 6, 4, 2):
            cosine = 1.0 - square * cosine * (1.0 / (power * (power - 1)))
        return 1.0 - 2.0 * sine * sine, 2.0 * sine * cosine

    @pl.loop(0, groups)
    def _(group):
        key = order_ref[group * slots]
        order = slot * groups + jnp.where(slot % 2 == 0, key, groups - 1 - key)
        cosine, sine = circle(order * lane)
        turn_cosine, turn_sine = circle(order * LANES)
        row = pl.multiple_of(group * 2 * pad_slots, 2 * pad_slots)
        for at in range(0, LON, LANES):
            width = min(LANES, LON - at)
            both = jnp.concatenate([cosine, -sine], axis=0).astype(jnp.bfloat16)
            table_ref[pl.ds(row, 2 * pad_slots), at : at + width] = both[:, :width]
            cosine, sine = (
                cosine * turn_cosine - sine * turn_sine,
                sine * turn_cosine + cosine * turn_sine,
            )


def weight_kernel(chan_in, rows_dev, items_ref, sum_ref):
    groups, rows, _ = items_ref.shape
    pad_slots = rows // 2
    total = items_ref[0].astype(jnp.float32)
    for group in range(1, groups):
        total = total + items_ref[group].astype(jnp.float32)
    head = LANES - chan_in
    lane = lax.broadcasted_iota(jnp.int32, (pad_slots, LANES), 1)
    near = pltpu.roll(total[:pad_slots], LANES - chan_in, 1)
    far = pltpu.roll(total[pad_slots:], LANES - (chan_in - head), 1)
    sum_ref[...] = jnp.where(lane < head, near, far)[:rows_dev, :chan_in]


def synthesis_kernel(items_ref, table_ref, field_ref):
    chan_in = field_ref.shape[0]
    groups, rows, _ = items_ref.shape
    items = items_ref[...].reshape(groups * rows, LANES)
    field = lax.dot_general(
        items, table_ref[...], (((0,), (0,)), ((), ())), preferred_element_type=jnp.float32
    )
    field_ref[...] = (field[:chan_in] * (1.0 / math.sqrt(LON))).astype(jnp.bfloat16)


def local(coef_grad, coef_saved, lift_weight, legendre, order_of_slot, trunc_degree):
    _, slots, _, embed, degrees = coef_grad.shape
    chan_in = coef_saved.shape[3]
    lats = legendre.shape[2]
    groups = lax.axis_size(GROUP_AXES)
    samples = lax.axis_size("chan")
    rows_dev = embed // groups
    pad_slots = max(round_up(slots, 8), round_up(rows_dev, 8))
    rows = 2 * pad_slots
    embed_tiles = embed // LANES
    tiles = lane_tiles(degrees)
    assert coef_grad.shape[0] == 1 and lats == groups and 2 * (LANES - chan_in) >= chan_in

    smem = pl.BlockSpec(memory_space=pltpu.SMEM)
    vmem = pl.BlockSpec(memory_space=pltpu.VMEM)
    hbm = pl.BlockSpec(memory_space=pltpu.HBM)
    grad_view = jnp.transpose(coef_grad[0], (0, 3, 1, 2))
    saved_view = jnp.transpose(coef_saved[0], (0, 2, 1, 3))
    packed = pl.pallas_call(
        lambda *refs: spectral_kernel(groups, pad_slots, *refs),
        out_shape=jax.ShapeDtypeStruct((groups, rows, LANES), jnp.bfloat16),
        in_specs=[hbm] * 6,
        out_specs=vmem,
        scratch_shapes=[
            pltpu.SMEM(order_of_slot.shape, jnp.int32),
            pltpu.SMEM(trunc_degree.shape, jnp.int32),
            pltpu.VMEM((slots, lats, degrees), jnp.bfloat16),
            pltpu.VMEM((chan_in, embed), jnp.bfloat16),
            pltpu.VMEM((slots, embed_tiles, round_up(2 * degrees, 16), LANES), jnp.bfloat16),
            *[pltpu.VMEM((slots, round_up(2 * chan_in, 16), width), jnp.bfloat16) for _, width in tiles],
            *[pltpu.VMEM((embed_tiles, 2 * round_up(degrees, LANES) + 8, LANES), jnp.float32)] * UNROLL,
            *[pltpu.VMEM((len(tiles), 2 * round_up(chan_in, 8) + 8, LANES), jnp.float32)] * UNROLL,
            pltpu.VMEM((UNROLL, len(tiles), lats, LANES), jnp.float32),
            pltpu.VMEM((rows * lats, embed), jnp.bfloat16),
            pltpu.VMEM(((rows + 1) * lats, LANES), jnp.float32),
            pltpu.VMEM((LANES, embed), jnp.float32),
            pltpu.VMEM((embed, LANES), jnp.float32),
            pltpu.SemaphoreType.DMA((4,)),
            pltpu.SemaphoreType.DMA((slots, embed_tiles)),
            pltpu.SemaphoreType.DMA((slots, len(tiles))),
        ],
        compiler_params=pltpu.CompilerParams(vmem_limit_bytes=60 << 20),
        name="spectral",
    )(order_of_slot, trunc_degree, grad_view, saved_view, jnp.transpose(legendre, (0, 2, 1)), lift_weight.T)

    received = lax.all_to_all(packed, GROUP_AXES, split_axis=0, concat_axis=0, tiled=True)

    table = pl.pallas_call(
        lambda *refs: table_kernel(groups, slots, *refs),
        out_shape=jax.ShapeDtypeStruct((groups * rows, LON), jnp.bfloat16),
        in_specs=[smem],
        out_specs=vmem,
        cost_estimate=pl.CostEstimate(flops=20_000_000, bytes_accessed=groups * rows * LON * 2, transcendentals=0),
        name="table",
    )(order_of_slot)

    own = pl.pallas_call(
        lambda *refs: weight_kernel(chan_in, rows_dev, *refs),
        out_shape=jax.ShapeDtypeStruct((rows_dev, chan_in), jnp.float32),
        in_specs=[vmem],
        out_specs=vmem,
        name="weight_rows",
    )(received)
    if samples == 2:
        weight_grad = own + lax.ppermute(own, "chan", [(0, 1), (1, 0)])
    else:
        weight_grad = lax.psum(own, "chan")

    field = pl.pallas_call(
        synthesis_kernel,
        out_shape=jax.ShapeDtypeStruct((chan_in, LON), jnp.bfloat16),
        in_specs=[vmem, vmem],
        out_specs=vmem,
        cost_estimate=pl.CostEstimate(flops=2 * groups * rows * LANES * LON, bytes_accessed=groups * rows * LON * 2, transcendentals=0),
        name="synthesis",
    )(received, table)
    return (field[None, :, None, :], weight_grad)


def solution(mesh):
    return jax.shard_map(
        local,
        mesh=mesh,
        in_specs=(
            P("chan", GROUP_AXES, None, None, None),
            P("chan", GROUP_AXES, None, None, None),
            P(),
            P(GROUP_AXES, None, None),
            P(),
            P("chan"),
        ),
        out_specs=(P("chan", None, GROUP_AXES, None), P(GROUP_AXES, None)),
        check_vma=False,
    )
```

```python
import math

import jax
import jax.numpy as jnp
from jax import lax
from jax.experimental import pallas as pl
from jax.experimental.pallas import tpu as pltpu
from jax.sharding import PartitionSpec as P

LON = 1440
LANES = 128
UNROLL = 4
SMALL_VMEM = 16 << 20
GROUP_AXES = ("order", "band")


def round_up(value, step):
    return -(-value // step) * step


def slot_classes(slots, groups, degrees):
    classes = {}
    for slot in range(slots):
        low = groups * slot
        if low < degrees:
            classes.setdefault(low // LANES, []).append(slot)
    return [(tile, found[0], found[-1] + 1) for tile, found in sorted(classes.items())]


def lane_tiles(degrees):
    return [(at, min(LANES, degrees - at)) for at in range(0, degrees, LANES)]


def spectral_kernel(groups, pad_slots, order_hbm, trunc_hbm, grad_hbm, saved_hbm, legendre_hbm, weight_hbm,
                    out_ref, order_ref, trunc_ref, legendre_buf, weight_buf, grad_buf, *rest):
    slots, degrees, _, embed = grad_hbm.shape
    chan_in = weight_hbm.shape[0]
    chan_pad = round_up(chan_in, 8)
    lats = legendre_hbm.shape[1]
    tiles = lane_tiles(degrees)
    saved_bufs = rest[: len(tiles)]
    grad_wides = rest[len(tiles) : len(tiles) + UNROLL]
    saved_wides = rest[len(tiles) + UNROLL : len(tiles) + 2 * UNROLL]
    legendre_wide, tilted, spec_wide, weight_acc, weight_turned, small_sem, grad_sem, saved_sem = rest[len(tiles) + 2 * UNROLL :]
    grad_pairs = grad_hbm.reshape(slots, 2 * degrees, embed)
    saved_pairs = saved_hbm.reshape(slots, 2 * chan_in, degrees)
    small_copies = [
        pltpu.make_async_copy(source, target, small_sem.at[at])
        for at, (source, target) in enumerate([
            (order_hbm, order_ref), (trunc_hbm, trunc_ref), (legendre_hbm, legendre_buf), (weight_hbm, weight_buf)
        ])
    ]
    for copy in small_copies:
        copy.start()
    embed_tiles = embed // LANES
    classes = slot_classes(slots, groups, degrees)[::-1]

    def grad_copies(slot, tile):
        rows = pl.ds(2 * tile * LANES, 2 * (degrees - tile * LANES))
        return [
            pltpu.make_async_copy(
                grad_pairs.at[slot, rows, pl.ds(at * LANES, LANES)],
                grad_buf.at[slot, at, rows],
                grad_sem.at[slot, at],
            )
            for at in range(embed_tiles)
        ]

    def saved_copies(slot, tile):
        return [
            pltpu.make_async_copy(
                saved_pairs.at[slot, :, pl.ds(*tiles[at])],
                saved_bufs[at].at[slot, pl.ds(0, 2 * chan_in)],
                saved_sem.at[slot, at],
            )
            for at in range(tile, len(tiles))
        ]

    for tile, first, last in classes:
        @pl.loop(first, last)
        def _(slot):
            for copy in grad_copies(slot, tile) + saved_copies(slot, tile):
                copy.start()

    weight_acc[...] = jnp.zeros_like(weight_acc)
    tilted[...] = jnp.zeros_like(tilted)
    for wide in grad_wides:
        for at in range(embed_tiles):
            edge = 2 * degrees // 8 * 8
            wide[at, edge:] = jnp.zeros((wide.shape[1] - edge, LANES), jnp.float32)
    for copy in small_copies:
        copy.wait()
    first_slot = (lax.axis_index("order") * lax.axis_size("band") + lax.axis_index("band")) * slots
    top = trunc_ref[0]

    def run(slot_ids, tile):
        low = tile * LANES
        live = degrees - low
        live_pad = round_up(live, LANES)
        for slot in slot_ids:
            for copy in grad_copies(slot, tile) + saved_copies(slot, tile):
                copy.wait()
        total = None
        for at_slot, slot in enumerate(slot_ids):
            grad_wide, saved_wide = grad_wides[at_slot], saved_wides[at_slot]
            order = order_ref[first_slot + slot]
            degree = lax.broadcasted_iota(jnp.int32, (1, live_pad), 1) + low
            mask = (degree >= order) & (degree <= top)
            for at in range(embed_tiles):
                pairs = grad_buf[slot, at, 2 * low : 2 * degrees]
                grad_wide[at, : 2 * live] = pairs.astype(jnp.float32)
            for at in range(tile, len(tiles)):
                start, width = tiles[at]
                pairs = saved_bufs[at][slot, : 2 * chan_in]
                saved_wide[at, : 2 * chan_in, :width] = pairs.astype(jnp.float32)
                legendre_wide[at_slot, at, :, :width] = legendre_buf[slot, :, start : start + width].astype(jnp.float32)
            for part in range(2):
                grads = jnp.concatenate(
                    [grad_wide[at, pl.ds(part, live_pad, stride=2)].astype(jnp.bfloat16) for at in range(embed_tiles)],
                    axis=1,
                )
                left = jnp.concatenate(
                    [
                        jnp.concatenate(
                            [legendre_wide[at_slot, at], saved_wide[at, pl.ds(part, chan_pad, stride=2)]], axis=0
                        )
                        for at in range(tile, len(tiles))
                    ],
                    axis=1,
                )
                left = jnp.where(mask, left, 0.0).astype(jnp.bfloat16)
                both = jnp.dot(left, grads, preferred_element_type=jnp.float32)
                row = pl.multiple_of((part * pad_slots + slot) * lats, lats)
                tilted[pl.ds(row, lats)] = both[:lats].astype(jnp.bfloat16)
                total = both[lats:] if total is None else total + both[lats:]
        weight_acc[:chan_pad] += total

    for tile, first, last in classes:
        count = len(grad_wides)
        chunks = (last - first) // count

        @pl.loop(0, chunks)
        def _(chunk):
            run([first + chunk * count + at for at in range(count)], tile)

        if first + chunks * count < last:
            run(list(range(first + chunks * count, last)), tile)

    spec_wide[pl.ds(0, tilted.shape[0]), :chan_in] = lax.dot_general(
        tilted[...], weight_buf[...], (((1,), (1,)), ((), ())), preferred_element_type=jnp.float32
    )
    for at in range(embed_tiles):
        weight_turned[at * LANES : (at + 1) * LANES] = weight_acc[:, at * LANES : (at + 1) * LANES].T
    rows_dev = embed // groups
    head = LANES - chan_in
    lane = lax.broadcasted_iota(jnp.int32, (2 * pad_slots, LANES), 1)
    for group in range(groups):
        block = weight_turned[group * rows_dev : (group + 1) * rows_dev]
        shifted = [pltpu.roll(block, chan_in, 1), pltpu.roll(block, chan_in - head, 1)]
        if rows_dev < pad_slots:
            fill = jnp.zeros((pad_slots - rows_dev, LANES), jnp.float32)
            shifted = [shifted[0], fill, shifted[1], fill]
        spec = spec_wide[pl.ds(group, 2 * pad_slots, stride=lats)]
        both = jnp.where(lane < chan_in, spec, jnp.concatenate(shifted, axis=0))
        out_ref[group] = both.astype(jnp.bfloat16)


def table_kernel(groups, slots, order_ref, table_ref):
    pad_slots = table_ref.shape[0] // (2 * groups)
    shape = (pad_slots, LANES)
    slot = lax.broadcasted_iota(jnp.int32, shape, 0)
    lane = lax.broadcasted_iota(jnp.int32, shape, 1)

    def circle(steps):
        steps = steps.astype(jnp.float32)
        turns = jnp.floor(steps * (1.0 / LON) + 0.5)
        half = (steps - turns * LON) * (math.pi / LON)
        square = half * half
        sine = 1.0
        for power in (11, 9, 7, 5, 3):
            sine = 1.0 - square * sine * (1.0 / (power * (power - 1)))
        sine = sine * half
        cosine = 1.0
        for power in (12, 10, 8, 6, 4, 2):
            cosine = 1.0 - square * cosine * (1.0 / (power * (power - 1)))
        return 1.0 - 2.0 * sine * sine, 2.0 * sine * cosine

    @pl.loop(0, groups)
    def _(group):
        key = order_ref[group * slots]
        order = slot * groups + jnp.where(slot % 2 == 0, key, groups - 1 - key)
        cosine, sine = circle(order * lane)
        turn_cosine, turn_sine = circle(order * LANES)
        row = pl.multiple_of(group * 2 * pad_slots, 2 * pad_slots)
        for at in range(0, LON, LANES):
            width = min(LANES, LON - at)
            both = jnp.concatenate([cosine, -sine], axis=0).astype(jnp.bfloat16)
            table_ref[pl.ds(row, 2 * pad_slots), at : at + width] = both[:, :width]
            cosine, sine = (
                cosine * turn_cosine - sine * turn_sine,
                sine * turn_cosine + cosine * turn_sine,
            )


def weight_kernel(chan_in, rows_dev, items_ref, sum_ref):
    groups, rows, _ = items_ref.shape
    pad_slots = rows // 2
    total = items_ref[0].astype(jnp.float32)
    for group in range(1, groups):
        total = total + items_ref[group].astype(jnp.float32)
    head = LANES - chan_in
    lane = lax.broadcasted_iota(jnp.int32, (pad_slots, LANES), 1)
    near = pltpu.roll(total[:pad_slots], LANES - chan_in, 1)
    far = pltpu.roll(total[pad_slots:], LANES - (chan_in - head), 1)
    sum_ref[...] = jnp.where(lane < head, near, far)[:rows_dev, :chan_in]


def synthesis_kernel(items_ref, table_ref, field_ref):
    chan_in = field_ref.shape[0]
    groups, rows, _ = items_ref.shape
    items = items_ref[...].reshape(groups * rows, LANES)
    field = lax.dot_general(
        items, table_ref[...], (((0,), (0,)), ((), ())), preferred_element_type=jnp.float32
    )
    field_ref[...] = (field[:chan_in] * (1.0 / math.sqrt(LON))).astype(jnp.bfloat16)


def local(coef_grad, coef_saved, lift_weight, legendre, order_of_slot, trunc_degree):
    _, slots, _, embed, degrees = coef_grad.shape
    chan_in = coef_saved.shape[3]
    lats = legendre.shape[2]
    groups = lax.axis_size(GROUP_AXES)
    samples = lax.axis_size("chan")
    rows_dev = embed // groups
    pad_slots = max(round_up(slots, 8), round_up(rows_dev, 8))
    rows = 2 * pad_slots
    embed_tiles = embed // LANES
    tiles = lane_tiles(degrees)
    assert coef_grad.shape[0] == 1 and lats == groups and 2 * (LANES - chan_in) >= chan_in

    smem = pl.BlockSpec(memory_space=pltpu.SMEM)
    vmem = pl.BlockSpec(memory_space=pltpu.VMEM)
    hbm = pl.BlockSpec(memory_space=pltpu.HBM)
    grad_view = jnp.transpose(coef_grad[0], (0, 3, 1, 2))
    saved_view = jnp.transpose(coef_saved[0], (0, 2, 1, 3))
    packed = pl.pallas_call(
        lambda *refs: spectral_kernel(groups, pad_slots, *refs),
        out_shape=jax.ShapeDtypeStruct((groups, rows, LANES), jnp.bfloat16),
        in_specs=[hbm] * 6,
        out_specs=vmem,
        scratch_shapes=[
            pltpu.SMEM(order_of_slot.shape, jnp.int32),
            pltpu.SMEM(trunc_degree.shape, jnp.int32),
            pltpu.VMEM((slots, lats, degrees), jnp.bfloat16),
            pltpu.VMEM((chan_in, embed), jnp.bfloat16),
            pltpu.VMEM((slots, embed_tiles, round_up(2 * degrees, 16), LANES), jnp.bfloat16),
            *[pltpu.VMEM((slots, round_up(2 * chan_in, 16), width), jnp.bfloat16) for _, width in tiles],
            *[pltpu.VMEM((embed_tiles, 2 * round_up(degrees, LANES) + 8, LANES), jnp.float32)] * UNROLL,
            *[pltpu.VMEM((len(tiles), 2 * round_up(chan_in, 8) + 8, LANES), jnp.float32)] * UNROLL,
            pltpu.VMEM((UNROLL, len(tiles), lats, LANES), jnp.float32),
            pltpu.VMEM((rows * lats, embed), jnp.bfloat16),
            pltpu.VMEM(((rows + 1) * lats, LANES), jnp.float32),
            pltpu.VMEM((LANES, embed), jnp.float32),
            pltpu.VMEM((embed, LANES), jnp.float32),
            pltpu.SemaphoreType.DMA((4,)),
            pltpu.SemaphoreType.DMA((slots, embed_tiles)),
            pltpu.SemaphoreType.DMA((slots, len(tiles))),
        ],
        compiler_params=pltpu.CompilerParams(vmem_limit_bytes=60 << 20),
        name="spectral",
    )(order_of_slot, trunc_degree, grad_view, saved_view, jnp.transpose(legendre, (0, 2, 1)), lift_weight.T)

    received = lax.all_to_all(packed, GROUP_AXES, split_axis=0, concat_axis=0, tiled=True)

    table = pl.pallas_call(
        lambda *refs: table_kernel(groups, slots, *refs),
        out_shape=jax.ShapeDtypeStruct((groups * rows, LON), jnp.bfloat16),
        in_specs=[smem],
        out_specs=vmem,
        compiler_params=pltpu.CompilerParams(vmem_limit_bytes=SMALL_VMEM),
        cost_estimate=pl.CostEstimate(flops=20_000_000, bytes_accessed=groups * rows * LON * 2, transcendentals=0),
        name="table",
    )(order_of_slot)

    own = pl.pallas_call(
        lambda *refs: weight_kernel(chan_in, rows_dev, *refs),
        out_shape=jax.ShapeDtypeStruct((rows_dev, chan_in), jnp.float32),
        in_specs=[vmem],
        out_specs=vmem,
        compiler_params=pltpu.CompilerParams(vmem_limit_bytes=SMALL_VMEM),
        name="weight_rows",
    )(received)
    if samples == 2:
        weight_grad = own + lax.ppermute(own, "chan", [(0, 1), (1, 0)])
    else:
        weight_grad = lax.psum(own, "chan")

    field = pl.pallas_call(
        synthesis_kernel,
        out_shape=jax.ShapeDtypeStruct((chan_in, LON), jnp.bfloat16),
        in_specs=[vmem, vmem],
        out_specs=vmem,
        compiler_params=pltpu.CompilerParams(vmem_limit_bytes=SMALL_VMEM),
        cost_estimate=pl.CostEstimate(flops=2 * groups * rows * LANES * LON, bytes_accessed=groups * rows * LON * 2, transcendentals=0),
        name="synthesis",
    )(received, table)
    return (field[None, :, None, :], weight_grad)


def solution(mesh):
    return jax.shard_map(
        local,
        mesh=mesh,
        in_specs=(
            P("chan", GROUP_AXES, None, None, None),
            P("chan", GROUP_AXES, None, None, None),
            P(),
            P(GROUP_AXES, None, None),
            P(),
            P("chan"),
        ),
        out_specs=(P("chan", None, GROUP_AXES, None), P(GROUP_AXES, None)),
        check_vma=False,
    )
```

```python
import math

import jax
import jax.numpy as jnp
from jax import lax
from jax.experimental import pallas as pl
from jax.experimental.pallas import tpu as pltpu
from jax.sharding import PartitionSpec as P

LON = 1440
LANES = 128
UNROLL = 4
SMALL_VMEM = 16 << 20
GROUP_AXES = ("order", "band")


def round_up(value, step):
    return -(-value // step) * step


def slot_classes(slots, groups, degrees):
    classes = {}
    for slot in range(slots):
        low = groups * slot
        if low < degrees:
            classes.setdefault(low // LANES, []).append(slot)
    return [(tile, found[0], found[-1] + 1) for tile, found in sorted(classes.items())]


def lane_tiles(degrees):
    return [(at, min(LANES, degrees - at)) for at in range(0, degrees, LANES)]


def spectral_kernel(groups, pad_slots, order_hbm, trunc_hbm, grad_hbm, saved_hbm, legendre_hbm, weight_hbm,
                    out_ref, order_ref, trunc_ref, legendre_buf, weight_buf, grad_buf, *rest):
    slots, degrees, _, embed = grad_hbm.shape
    chan_in = weight_hbm.shape[0]
    chan_pad = round_up(chan_in, 8)
    lats = legendre_hbm.shape[1]
    tiles = lane_tiles(degrees)
    saved_bufs = rest[: len(tiles)]
    grad_wides = rest[len(tiles) : len(tiles) + UNROLL]
    saved_wides = rest[len(tiles) + UNROLL : len(tiles) + 2 * UNROLL]
    legendre_wide, tilted, spec_wide, weight_acc, weight_turned, small_sem, grad_sem, saved_sem = rest[len(tiles) + 2 * UNROLL :]
    grad_pairs = grad_hbm.reshape(slots, 2 * degrees, embed)
    saved_pairs = saved_hbm.reshape(slots, 2 * chan_in, degrees)
    small_copies = [
        pltpu.make_async_copy(source, target, small_sem.at[at])
        for at, (source, target) in enumerate([
            (order_hbm, order_ref), (trunc_hbm, trunc_ref), (legendre_hbm, legendre_buf), (weight_hbm, weight_buf)
        ])
    ]
    for copy in small_copies:
        copy.start()
    embed_tiles = embed // LANES
    classes = slot_classes(slots, groups, degrees)[::-1]

    def copies(slot, tile, turn):
        rows = pl.ds(2 * tile * LANES, 2 * (degrees - tile * LANES))
        return [
            pltpu.make_async_copy(
                grad_pairs.at[slot, rows, pl.ds(at * LANES, LANES)], grad_buf.at[slot, at, rows], grad_sem.at[turn]
            )
            for at in range(embed_tiles)
        ] + [
            pltpu.make_async_copy(
                saved_pairs.at[slot, :, pl.ds(*tiles[at])],
                saved_bufs[at].at[slot, pl.ds(0, 2 * chan_in)],
                saved_sem.at[turn, at],
            )
            for at in range(tile, len(tiles))
        ]

    def arrivals(first, count, tile, turn):
        span = pl.ds(first, count)
        rows = pl.ds(2 * tile * LANES, 2 * (degrees - tile * LANES))
        landed = [(grad_buf.at[span, :, rows], grad_sem.at[turn])] + [
            (saved_bufs[at].at[span, pl.ds(0, 2 * chan_in)], saved_sem.at[turn, at]) for at in range(tile, len(tiles))
        ]
        return [pltpu.make_async_copy(place, place, sem) for place, sem in landed]

    turn_of = 0
    for tile, first, last in classes:
        @pl.loop(first, last)
        def _(slot):
            for copy in copies(slot, tile, turn_of + lax.div(slot - first, UNROLL)):
                copy.start()

        turn_of += -(-(last - first) // UNROLL)

    weight_acc[...] = jnp.zeros_like(weight_acc)
    tilted[...] = jnp.zeros_like(tilted)
    for wide in grad_wides:
        for at in range(embed_tiles):
            edge = 2 * degrees // 8 * 8
            wide[at, edge:] = jnp.zeros((wide.shape[1] - edge, LANES), jnp.float32)
    for copy in small_copies:
        copy.wait()
    first_slot = (lax.axis_index("order") * lax.axis_size("band") + lax.axis_index("band")) * slots
    top = trunc_ref[0]

    def run(first_slot_id, count, tile, turn):
        slot_ids = [first_slot_id + at for at in range(count)]
        low = tile * LANES
        live = degrees - low
        live_pad = round_up(live, LANES)
        for copy in arrivals(first_slot_id, count, tile, turn):
            copy.wait()
        total = None
        for at_slot, slot in enumerate(slot_ids):
            grad_wide, saved_wide = grad_wides[at_slot], saved_wides[at_slot]
            order = order_ref[first_slot + slot]
            degree = lax.broadcasted_iota(jnp.int32, (1, live_pad), 1) + low
            mask = (degree >= order) & (degree <= top)
            for at in range(embed_tiles):
                pairs = grad_buf[slot, at, 2 * low : 2 * degrees]
                grad_wide[at, : 2 * live] = pairs.astype(jnp.float32)
            for at in range(tile, len(tiles)):
                start, width = tiles[at]
                pairs = saved_bufs[at][slot, : 2 * chan_in]
                saved_wide[at, : 2 * chan_in, :width] = pairs.astype(jnp.float32)
                legendre_wide[at_slot, at, :, :width] = legendre_buf[slot, :, start : start + width].astype(jnp.float32)
            for part in range(2):
                grads = jnp.concatenate(
                    [grad_wide[at, pl.ds(part, live_pad, stride=2)].astype(jnp.bfloat16) for at in range(embed_tiles)],
                    axis=1,
                )
                left = jnp.concatenate(
                    [
                        jnp.concatenate(
                            [legendre_wide[at_slot, at], saved_wide[at, pl.ds(part, chan_pad, stride=2)]], axis=0
                        )
                        for at in range(tile, len(tiles))
                    ],
                    axis=1,
                )
                left = jnp.where(mask, left, 0.0).astype(jnp.bfloat16)
                both = jnp.dot(left, grads, preferred_element_type=jnp.float32)
                row = pl.multiple_of((part * pad_slots + slot) * lats, lats)
                tilted[pl.ds(row, lats)] = both[:lats].astype(jnp.bfloat16)
                total = both[lats:] if total is None else total + both[lats:]
        weight_acc[:chan_pad] += total

    turn_of = 0
    for tile, first, last in classes:
        chunks = (last - first) // UNROLL

        @pl.loop(0, chunks)
        def _(chunk):
            run(first + chunk * UNROLL, UNROLL, tile, turn_of + chunk)

        turn_of += chunks
        if first + chunks * UNROLL < last:
            run(first + chunks * UNROLL, last - first - chunks * UNROLL, tile, turn_of)
            turn_of += 1

    spec_wide[pl.ds(0, tilted.shape[0]), :chan_in] = lax.dot_general(
        tilted[...], weight_buf[...], (((1,), (1,)), ((), ())), preferred_element_type=jnp.float32
    )
    for at in range(embed_tiles):
        weight_turned[at * LANES : (at + 1) * LANES] = weight_acc[:, at * LANES : (at + 1) * LANES].T
    rows_dev = embed // groups
    head = LANES - chan_in
    lane = lax.broadcasted_iota(jnp.int32, (2 * pad_slots, LANES), 1)
    for group in range(groups):
        block = weight_turned[group * rows_dev : (group + 1) * rows_dev]
        shifted = [pltpu.roll(block, chan_in, 1), pltpu.roll(block, chan_in - head, 1)]
        if rows_dev < pad_slots:
            fill = jnp.zeros((pad_slots - rows_dev, LANES), jnp.float32)
            shifted = [shifted[0], fill, shifted[1], fill]
        spec = spec_wide[pl.ds(group, 2 * pad_slots, stride=lats)]
        both = jnp.where(lane < chan_in, spec, jnp.concatenate(shifted, axis=0))
        out_ref[group] = both.astype(jnp.bfloat16)


def table_kernel(groups, slots, order_ref, table_ref):
    pad_slots = table_ref.shape[0] // (2 * groups)
    shape = (pad_slots, LANES)
    slot = lax.broadcasted_iota(jnp.int32, shape, 0)
    lane = lax.broadcasted_iota(jnp.int32, shape, 1)

    def circle(steps):
        steps = steps.astype(jnp.float32)
        turns = jnp.floor(steps * (1.0 / LON) + 0.5)
        half = (steps - turns * LON) * (math.pi / LON)
        square = half * half
        sine = 1.0
        for power in (11, 9, 7, 5, 3):
            sine = 1.0 - square * sine * (1.0 / (power * (power - 1)))
        sine = sine * half
        cosine = 1.0
        for power in (12, 10, 8, 6, 4, 2):
            cosine = 1.0 - square * cosine * (1.0 / (power * (power - 1)))
        return 1.0 - 2.0 * sine * sine, 2.0 * sine * cosine

    @pl.loop(0, groups)
    def _(group):
        key = order_ref[group * slots]
        order = slot * groups + jnp.where(slot % 2 == 0, key, groups - 1 - key)
        cosine, sine = circle(order * lane)
        turn_cosine, turn_sine = circle(order * LANES)
        row = pl.multiple_of(group * 2 * pad_slots, 2 * pad_slots)
        for at in range(0, LON, LANES):
            width = min(LANES, LON - at)
            both = jnp.concatenate([cosine, -sine], axis=0).astype(jnp.bfloat16)
            table_ref[pl.ds(row, 2 * pad_slots), at : at + width] = both[:, :width]
            cosine, sine = (
                cosine * turn_cosine - sine * turn_sine,
                sine * turn_cosine + cosine * turn_sine,
            )


def weight_kernel(chan_in, rows_dev, items_ref, sum_ref):
    groups, rows, _ = items_ref.shape
    pad_slots = rows // 2
    total = items_ref[0].astype(jnp.float32)
    for group in range(1, groups):
        total = total + items_ref[group].astype(jnp.float32)
    head = LANES - chan_in
    lane = lax.broadcasted_iota(jnp.int32, (pad_slots, LANES), 1)
    near = pltpu.roll(total[:pad_slots], LANES - chan_in, 1)
    far = pltpu.roll(total[pad_slots:], LANES - (chan_in - head), 1)
    sum_ref[...] = jnp.where(lane < head, near, far)[:rows_dev, :chan_in]


def synthesis_kernel(items_ref, table_ref, field_ref):
    chan_in = field_ref.shape[0]
    groups, rows, _ = items_ref.shape
    items = items_ref[...].reshape(groups * rows, LANES)
    field = lax.dot_general(
        items, table_ref[...], (((0,), (0,)), ((), ())), preferred_element_type=jnp.float32
    )
    field_ref[...] = (field[:chan_in] * (1.0 / math.sqrt(LON))).astype(jnp.bfloat16)


def local(coef_grad, coef_saved, lift_weight, legendre, order_of_slot, trunc_degree):
    _, slots, _, embed, degrees = coef_grad.shape
    chan_in = coef_saved.shape[3]
    lats = legendre.shape[2]
    groups = lax.axis_size(GROUP_AXES)
    samples = lax.axis_size("chan")
    rows_dev = embed // groups
    pad_slots = max(round_up(slots, 8), round_up(rows_dev, 8))
    rows = 2 * pad_slots
    embed_tiles = embed // LANES
    tiles = lane_tiles(degrees)
    turns = sum(-(-(last - first) // UNROLL) for _, first, last in slot_classes(slots, groups, degrees))
    assert coef_grad.shape[0] == 1 and lats == groups and 2 * (LANES - chan_in) >= chan_in

    smem = pl.BlockSpec(memory_space=pltpu.SMEM)
    vmem = pl.BlockSpec(memory_space=pltpu.VMEM)
    hbm = pl.BlockSpec(memory_space=pltpu.HBM)
    grad_view = jnp.transpose(coef_grad[0], (0, 3, 1, 2))
    saved_view = jnp.transpose(coef_saved[0], (0, 2, 1, 3))
    packed = pl.pallas_call(
        lambda *refs: spectral_kernel(groups, pad_slots, *refs),
        out_shape=jax.ShapeDtypeStruct((groups, rows, LANES), jnp.bfloat16),
        in_specs=[hbm] * 6,
        out_specs=vmem,
        scratch_shapes=[
            pltpu.SMEM(order_of_slot.shape, jnp.int32),
            pltpu.SMEM(trunc_degree.shape, jnp.int32),
            pltpu.VMEM((slots, lats, degrees), jnp.bfloat16),
            pltpu.VMEM((chan_in, embed), jnp.bfloat16),
            pltpu.VMEM((slots, embed_tiles, round_up(2 * degrees, 16), LANES), jnp.bfloat16),
            *[pltpu.VMEM((slots, round_up(2 * chan_in, 16), width), jnp.bfloat16) for _, width in tiles],
            *[pltpu.VMEM((embed_tiles, 2 * round_up(degrees, LANES) + 8, LANES), jnp.float32)] * UNROLL,
            *[pltpu.VMEM((len(tiles), 2 * round_up(chan_in, 8) + 8, LANES), jnp.float32)] * UNROLL,
            pltpu.VMEM((UNROLL, len(tiles), lats, LANES), jnp.float32),
            pltpu.VMEM((rows * lats, embed), jnp.bfloat16),
            pltpu.VMEM(((rows + 1) * lats, LANES), jnp.float32),
            pltpu.VMEM((LANES, embed), jnp.float32),
            pltpu.VMEM((embed, LANES), jnp.float32),
            pltpu.SemaphoreType.DMA((4,)),
            pltpu.SemaphoreType.DMA((turns,)),
            pltpu.SemaphoreType.DMA((turns, len(tiles))),
        ],
        compiler_params=pltpu.CompilerParams(vmem_limit_bytes=60 << 20),
        name="spectral",
    )(order_of_slot, trunc_degree, grad_view, saved_view, jnp.transpose(legendre, (0, 2, 1)), lift_weight.T)

    received = lax.all_to_all(packed, GROUP_AXES, split_axis=0, concat_axis=0, tiled=True)

    table = pl.pallas_call(
        lambda *refs: table_kernel(groups, slots, *refs),
        out_shape=jax.ShapeDtypeStruct((groups * rows, LON), jnp.bfloat16),
        in_specs=[smem],
        out_specs=vmem,
        compiler_params=pltpu.CompilerParams(vmem_limit_bytes=SMALL_VMEM),
        cost_estimate=pl.CostEstimate(flops=20_000_000, bytes_accessed=groups * rows * LON * 2, transcendentals=0),
        name="table",
    )(order_of_slot)

    own = pl.pallas_call(
        lambda *refs: weight_kernel(chan_in, rows_dev, *refs),
        out_shape=jax.ShapeDtypeStruct((rows_dev, chan_in), jnp.float32),
        in_specs=[vmem],
        out_specs=vmem,
        compiler_params=pltpu.CompilerParams(vmem_limit_bytes=SMALL_VMEM),
        name="weight_rows",
    )(received)
    if samples == 2:
        weight_grad = own + lax.ppermute(own, "chan", [(0, 1), (1, 0)])
    else:
        weight_grad = lax.psum(own, "chan")

    field = pl.pallas_call(
        synthesis_kernel,
        out_shape=jax.ShapeDtypeStruct((chan_in, LON), jnp.bfloat16),
        in_specs=[vmem, vmem],
        out_specs=vmem,
        compiler_params=pltpu.CompilerParams(vmem_limit_bytes=SMALL_VMEM),
        cost_estimate=pl.CostEstimate(flops=2 * groups * rows * LANES * LON, bytes_accessed=groups * rows * LON * 2, transcendentals=0),
        name="synthesis",
    )(received, table)
    return (field[None, :, None, :], weight_grad)


def solution(mesh):
    return jax.shard_map(
        local,
        mesh=mesh,
        in_specs=(
            P("chan", GROUP_AXES, None, None, None),
            P("chan", GROUP_AXES, None, None, None),
            P(),
            P(GROUP_AXES, None, None),
            P(),
            P("chan"),
        ),
        out_specs=(P("chan", None, GROUP_AXES, None), P(GROUP_AXES, None)),
        check_vma=False,
    )
```

```python
import math

import jax
import jax.numpy as jnp
from jax import lax
from jax.experimental import pallas as pl
from jax.experimental.pallas import tpu as pltpu
from jax.sharding import PartitionSpec as P

LON = 1440
LANES = 128
UNROLL = 4
SMALL_VMEM = 16 << 20
GROUP_AXES = ("order", "band")


def round_up(value, step):
    return -(-value // step) * step


def slot_classes(slots, groups, degrees):
    classes = {}
    for slot in range(slots):
        low = groups * slot
        if low < degrees:
            classes.setdefault(low // LANES, []).append(slot)
    return [(tile, found[0], found[-1] + 1) for tile, found in sorted(classes.items())]


def lane_tiles(degrees):
    return [(at, min(LANES, degrees - at)) for at in range(0, degrees, LANES)]


def spectral_kernel(groups, pad_slots, order_hbm, trunc_hbm, grad_hbm, saved_hbm, legendre_hbm, weight_hbm,
                    out_ref, order_ref, trunc_ref, legendre_buf, weight_buf, grad_buf, *rest):
    slots, degrees, _, embed = grad_hbm.shape
    chan_in = weight_hbm.shape[0]
    chan_pad = round_up(chan_in, 8)
    lats = legendre_hbm.shape[1]
    tiles = lane_tiles(degrees)
    saved_bufs = rest[: len(tiles)]
    grad_wides = rest[len(tiles) : len(tiles) + UNROLL]
    saved_wides = rest[len(tiles) + UNROLL : len(tiles) + 2 * UNROLL]
    legendre_wide, tilted, spec_wide, weight_acc, weight_turned, small_sem, grad_sem, saved_sem = rest[len(tiles) + 2 * UNROLL :]
    grad_pairs = grad_hbm.reshape(slots, 2 * degrees, embed)
    saved_pairs = saved_hbm.reshape(slots, 2 * chan_in, degrees)
    small_copies = [
        pltpu.make_async_copy(source, target, small_sem.at[at])
        for at, (source, target) in enumerate([
            (order_hbm, order_ref), (trunc_hbm, trunc_ref), (legendre_hbm, legendre_buf), (weight_hbm, weight_buf)
        ])
    ]
    for copy in small_copies:
        copy.start()
    embed_tiles = embed // LANES
    classes = slot_classes(slots, groups, degrees)[::-1]

    def copies(slot, tile, turn):
        rows = pl.ds(2 * tile * LANES, 2 * (degrees - tile * LANES))
        return [
            pltpu.make_async_copy(
                grad_pairs.at[slot, rows, pl.ds(at * LANES, LANES)], grad_buf.at[slot, at, rows], grad_sem.at[turn]
            )
            for at in range(embed_tiles)
        ] + [
            pltpu.make_async_copy(
                saved_pairs.at[slot, :, pl.ds(*tiles[at])],
                saved_bufs[at].at[slot, pl.ds(0, 2 * chan_in)],
                saved_sem.at[turn, at],
            )
            for at in range(tile, len(tiles))
        ]

    def arrivals(first, count, tile, turn):
        span = pl.ds(first, count)
        rows = pl.ds(2 * tile * LANES, 2 * (degrees - tile * LANES))
        landed = [(grad_buf.at[span, :, rows], grad_sem.at[turn])] + [
            (saved_bufs[at].at[span, pl.ds(0, 2 * chan_in)], saved_sem.at[turn, at]) for at in range(tile, len(tiles))
        ]
        return [pltpu.make_async_copy(place, place, sem) for place, sem in landed]

    turn_of = 0
    for tile, first, last in classes:
        @pl.loop(first, last)
        def _(slot):
            for copy in copies(slot, tile, turn_of + lax.div(slot - first, UNROLL)):
                copy.start()

        turn_of += -(-(last - first) // UNROLL)

    weight_acc[...] = jnp.zeros_like(weight_acc)
    filled = max(last for _, _, last in classes)
    for part in range(2):
        start, stop = (part * pad_slots + filled) * lats, (part + 1) * pad_slots * lats
        if start < stop:
            tilted[start:stop] = jnp.zeros((stop - start, embed), jnp.bfloat16)
    for wide in grad_wides:
        for at in range(embed_tiles):
            edge = 2 * degrees // 8 * 8
            wide[at, edge:] = jnp.zeros((wide.shape[1] - edge, LANES), jnp.float32)
    for copy in small_copies:
        copy.wait()
    first_slot = (lax.axis_index("order") * lax.axis_size("band") + lax.axis_index("band")) * slots
    top = trunc_ref[0]

    def run(first_slot_id, count, tile, turn):
        slot_ids = [first_slot_id + at for at in range(count)]
        low = tile * LANES
        live = degrees - low
        live_pad = round_up(live, LANES)
        for copy in arrivals(first_slot_id, count, tile, turn):
            copy.wait()
        total = None
        for at_slot, slot in enumerate(slot_ids):
            grad_wide, saved_wide = grad_wides[at_slot], saved_wides[at_slot]
            order = order_ref[first_slot + slot]
            degree = lax.broadcasted_iota(jnp.int32, (1, live_pad), 1) + low
            mask = (degree >= order) & (degree <= top)
            for at in range(embed_tiles):
                pairs = grad_buf[slot, at, 2 * low : 2 * degrees]
                grad_wide[at, : 2 * live] = pairs.astype(jnp.float32)
            for at in range(tile, len(tiles)):
                start, width = tiles[at]
                pairs = saved_bufs[at][slot, : 2 * chan_in]
                saved_wide[at, : 2 * chan_in, :width] = pairs.astype(jnp.float32)
                legendre_wide[at_slot, at, :, :width] = legendre_buf[slot, :, start : start + width].astype(jnp.float32)
            for part in range(2):
                grads = jnp.concatenate(
                    [grad_wide[at, pl.ds(part, live_pad, stride=2)].astype(jnp.bfloat16) for at in range(embed_tiles)],
                    axis=1,
                )
                left = jnp.concatenate(
                    [
                        jnp.concatenate(
                            [legendre_wide[at_slot, at], saved_wide[at, pl.ds(part, chan_pad, stride=2)]], axis=0
                        )
                        for at in range(tile, len(tiles))
                    ],
                    axis=1,
                )
                left = jnp.where(mask, left, 0.0).astype(jnp.bfloat16)
                both = jnp.dot(left, grads, preferred_element_type=jnp.float32)
                row = pl.multiple_of((part * pad_slots + slot) * lats, lats)
                tilted[pl.ds(row, lats)] = both[:lats].astype(jnp.bfloat16)
                total = both[lats:] if total is None else total + both[lats:]
        weight_acc[:chan_pad] += total

    turn_of = 0
    for tile, first, last in classes:
        chunks = (last - first) // UNROLL

        @pl.loop(0, chunks)
        def _(chunk):
            run(first + chunk * UNROLL, UNROLL, tile, turn_of + chunk)

        turn_of += chunks
        if first + chunks * UNROLL < last:
            run(first + chunks * UNROLL, last - first - chunks * UNROLL, tile, turn_of)
            turn_of += 1

    spec_wide[pl.ds(0, tilted.shape[0]), :chan_in] = lax.dot_general(
        tilted[...], weight_buf[...], (((1,), (1,)), ((), ())), preferred_element_type=jnp.float32
    )
    for at in range(embed_tiles):
        weight_turned[at * LANES : (at + 1) * LANES] = weight_acc[:, at * LANES : (at + 1) * LANES].T
    rows_dev = embed // groups
    head = LANES - chan_in
    lane = lax.broadcasted_iota(jnp.int32, (2 * pad_slots, LANES), 1)
    for group in range(groups):
        block = weight_turned[group * rows_dev : (group + 1) * rows_dev]
        shifted = [pltpu.roll(block, chan_in, 1), pltpu.roll(block, chan_in - head, 1)]
        if rows_dev < pad_slots:
            fill = jnp.zeros((pad_slots - rows_dev, LANES), jnp.float32)
            shifted = [shifted[0], fill, shifted[1], fill]
        spec = spec_wide[pl.ds(group, 2 * pad_slots, stride=lats)]
        both = jnp.where(lane < chan_in, spec, jnp.concatenate(shifted, axis=0))
        out_ref[group] = both.astype(jnp.bfloat16)


def table_kernel(groups, slots, order_ref, table_ref):
    pad_slots = table_ref.shape[0] // (2 * groups)
    shape = (pad_slots, LANES)
    slot = lax.broadcasted_iota(jnp.int32, shape, 0)
    lane = lax.broadcasted_iota(jnp.int32, shape, 1)

    def circle(steps):
        steps = steps.astype(jnp.float32)
        turns = jnp.floor(steps * (1.0 / LON) + 0.5)
        half = (steps - turns * LON) * (math.pi / LON)
        square = half * half
        sine = 1.0
        for power in (11, 9, 7, 5, 3):
            sine = 1.0 - square * sine * (1.0 / (power * (power - 1)))
        sine = sine * half
        cosine = 1.0
        for power in (12, 10, 8, 6, 4, 2):
            cosine = 1.0 - square * cosine * (1.0 / (power * (power - 1)))
        return 1.0 - 2.0 * sine * sine, 2.0 * sine * cosine

    @pl.loop(0, groups)
    def _(group):
        key = order_ref[group * slots]
        order = slot * groups + jnp.where(slot % 2 == 0, key, groups - 1 - key)
        cosine, sine = circle(order * lane)
        turn_cosine, turn_sine = circle(order * LANES)
        row = pl.multiple_of(group * 2 * pad_slots, 2 * pad_slots)
        for at in range(0, LON, LANES):
            width = min(LANES, LON - at)
            both = jnp.concatenate([cosine, -sine], axis=0).astype(jnp.bfloat16)
            table_ref[pl.ds(row, 2 * pad_slots), at : at + width] = both[:, :width]
            cosine, sine = (
                cosine * turn_cosine - sine * turn_sine,
                sine * turn_cosine + cosine * turn_sine,
            )


def weight_kernel(chan_in, rows_dev, items_ref, sum_ref):
    groups, rows, _ = items_ref.shape
    pad_slots = rows // 2
    total = items_ref[0].astype(jnp.float32)
    for group in range(1, groups):
        total = total + items_ref[group].astype(jnp.float32)
    head = LANES - chan_in
    lane = lax.broadcasted_iota(jnp.int32, (pad_slots, LANES), 1)
    near = pltpu.roll(total[:pad_slots], LANES - chan_in, 1)
    far = pltpu.roll(total[pad_slots:], LANES - (chan_in - head), 1)
    sum_ref[...] = jnp.where(lane < head, near, far)[:rows_dev, :chan_in]


def synthesis_kernel(items_ref, table_ref, field_ref):
    chan_in = field_ref.shape[0]
    groups, rows, _ = items_ref.shape
    items = items_ref[...].reshape(groups * rows, LANES)
    field = lax.dot_general(
        items, table_ref[...], (((0,), (0,)), ((), ())), preferred_element_type=jnp.float32
    )
    field_ref[...] = (field[:chan_in] * (1.0 / math.sqrt(LON))).astype(jnp.bfloat16)


def local(coef_grad, coef_saved, lift_weight, legendre, order_of_slot, trunc_degree):
    _, slots, _, embed, degrees = coef_grad.shape
    chan_in = coef_saved.shape[3]
    lats = legendre.shape[2]
    groups = lax.axis_size(GROUP_AXES)
    samples = lax.axis_size("chan")
    rows_dev = embed // groups
    pad_slots = max(round_up(slots, 8), round_up(rows_dev, 8))
    rows = 2 * pad_slots
    embed_tiles = embed // LANES
    tiles = lane_tiles(degrees)
    turns = sum(-(-(last - first) // UNROLL) for _, first, last in slot_classes(slots, groups, degrees))
    assert coef_grad.shape[0] == 1 and lats == groups and 2 * (LANES - chan_in) >= chan_in

    smem = pl.BlockSpec(memory_space=pltpu.SMEM)
    vmem = pl.BlockSpec(memory_space=pltpu.VMEM)
    hbm = pl.BlockSpec(memory_space=pltpu.HBM)
    grad_view = jnp.transpose(coef_grad[0], (0, 3, 1, 2))
    saved_view = jnp.transpose(coef_saved[0], (0, 2, 1, 3))
    packed = pl.pallas_call(
        lambda *refs: spectral_kernel(groups, pad_slots, *refs),
        out_shape=jax.ShapeDtypeStruct((groups, rows, LANES), jnp.bfloat16),
        in_specs=[hbm] * 6,
        out_specs=vmem,
        scratch_shapes=[
            pltpu.SMEM(order_of_slot.shape, jnp.int32),
            pltpu.SMEM(trunc_degree.shape, jnp.int32),
            pltpu.VMEM((slots, lats, degrees), jnp.bfloat16),
            pltpu.VMEM((chan_in, embed), jnp.bfloat16),
            pltpu.VMEM((slots, embed_tiles, round_up(2 * degrees, 16), LANES), jnp.bfloat16),
            *[pltpu.VMEM((slots, round_up(2 * chan_in, 16), width), jnp.bfloat16) for _, width in tiles],
            *[pltpu.VMEM((embed_tiles, 2 * round_up(degrees, LANES) + 8, LANES), jnp.float32)] * UNROLL,
            *[pltpu.VMEM((len(tiles), 2 * round_up(chan_in, 8) + 8, LANES), jnp.float32)] * UNROLL,
            pltpu.VMEM((UNROLL, len(tiles), lats, LANES), jnp.float32),
            pltpu.VMEM((rows * lats, embed), jnp.bfloat16),
            pltpu.VMEM(((rows + 1) * lats, LANES), jnp.float32),
            pltpu.VMEM((LANES, embed), jnp.float32),
            pltpu.VMEM((embed, LANES), jnp.float32),
            pltpu.SemaphoreType.DMA((4,)),
            pltpu.SemaphoreType.DMA((turns,)),
            pltpu.SemaphoreType.DMA((turns, len(tiles))),
        ],
        compiler_params=pltpu.CompilerParams(vmem_limit_bytes=60 << 20),
        name="spectral",
    )(order_of_slot, trunc_degree, grad_view, saved_view, jnp.transpose(legendre, (0, 2, 1)), lift_weight.T)

    received = lax.all_to_all(packed, GROUP_AXES, split_axis=0, concat_axis=0, tiled=True)

    table = pl.pallas_call(
        lambda *refs: table_kernel(groups, slots, *refs),
        out_shape=jax.ShapeDtypeStruct((groups * rows, LON), jnp.bfloat16),
        in_specs=[smem],
        out_specs=vmem,
        compiler_params=pltpu.CompilerParams(vmem_limit_bytes=SMALL_VMEM),
        cost_estimate=pl.CostEstimate(flops=20_000_000, bytes_accessed=groups * rows * LON * 2, transcendentals=0),
        name="table",
    )(order_of_slot)

    own = pl.pallas_call(
        lambda *refs: weight_kernel(chan_in, rows_dev, *refs),
        out_shape=jax.ShapeDtypeStruct((rows_dev, chan_in), jnp.float32),
        in_specs=[vmem],
        out_specs=vmem,
        compiler_params=pltpu.CompilerParams(vmem_limit_bytes=SMALL_VMEM),
        name="weight_rows",
    )(received)
    if samples == 2:
        weight_grad = own + lax.ppermute(own, "chan", [(0, 1), (1, 0)])
    else:
        weight_grad = lax.psum(own, "chan")

    field = pl.pallas_call(
        synthesis_kernel,
        out_shape=jax.ShapeDtypeStruct((chan_in, LON), jnp.bfloat16),
        in_specs=[vmem, vmem],
        out_specs=vmem,
        compiler_params=pltpu.CompilerParams(vmem_limit_bytes=SMALL_VMEM),
        cost_estimate=pl.CostEstimate(flops=2 * groups * rows * LANES * LON, bytes_accessed=groups * rows * LON * 2, transcendentals=0),
        name="synthesis",
    )(received, table)
    return (field[None, :, None, :], weight_grad)


def solution(mesh):
    return jax.shard_map(
        local,
        mesh=mesh,
        in_specs=(
            P("chan", GROUP_AXES, None, None, None),
            P("chan", GROUP_AXES, None, None, None),
            P(),
            P(GROUP_AXES, None, None),
            P(),
            P("chan"),
        ),
        out_specs=(P("chan", None, GROUP_AXES, None), P(GROUP_AXES, None)),
        check_vma=False,
    )
```
